1024 devices in a mesh: segment: 64 (over y, z), row: 4 (over x_hi), col: 4 (over x_lo, core).
Axes of the slice: x: 8 (x_hi: 4, x_lo: 2; x = x_hi * 2 + x_lo), y: 8, z: 8, core: 2. Of those that a mesh axis runs over, the one named last changes fastest.
Arguments:
- weights: bfloat16 [64, 4096, 4096], P('segment', 'row', 'col'), may hold values from -0.09375 to 0.09375
- layer_gains: float32 [64, 4096], P('segment', 'col'), may hold values from -0.5 to 0.5
- incoming: bfloat16 [64, 256, 4096], P('segment', 'row', 'col'), may hold values from -6 to 6
- fresh_batch: bfloat16 [256, 4096], P('row', 'col'), may hold values from -6 to 6
- returning: bfloat16 [64, 256, 4096], P('segment', 'row', 'col'), may hold values from -6 to 6
- fresh_cotangent: bfloat16 [256, 4096], P('row', 'col'), may hold values from -6 to 6
- stashed_inputs: bfloat16 [64, 2, 256, 4096], P('segment', None, 'row', 'col'), may hold values from -6 to 6
Outputs:
- layer_outputs: bfloat16 [64, 2, 256, 4096], P('segment', None, 'row', 'col')
- input_grads: bfloat16 [64, 2, 256, 4096], P('segment', None, 'row', 'col')
The draws below stay inside these ranges and needn't reach their ends.
All inputs are finite; a program needn't handle non-finite values.
Results may differ from the reference program's by a relative error of at most 0.0055.
Values may be sent and summed in bfloat16 or wider, within the bound.
A program may use at most 32 MiB of HBM per device.

```python
import jax
import jax.numpy as jnp
from jax import lax

D = 4096
TOKENS_MB = 256
SEGMENTS = 64


def block_scale(key, shape, split, least, high):
    gain = 1.0
    for axis_at, parts in split:
        draws = jax.random.uniform(jax.random.fold_in(jax.random.fold_in(key, 6), axis_at), (parts,), jnp.float32, least / len(split), high / len(split))
        gain = gain * jnp.repeat(jnp.exp(draws), shape[axis_at] // parts).reshape((-1,) + (1,) * (len(shape) - 1 - axis_at))
    return gain


def scatter_about(stream_key, dims, deviation, limit, split=(), dtype=jnp.bfloat16):
    level = block_scale(stream_key, dims, split, -0.22, 0.18) if split else 1.0
    drawn = jax.random.normal(stream_key, dims, jnp.float32) * deviation * level
    return jnp.minimum(jnp.maximum(drawn, -limit), limit).astype(dtype)


def setup_inputs(seed: int = 0) -> dict:
    arg_keys = jax.random.split(jax.random.key(seed), 8)
    weights = scatter_about(arg_keys[0], (SEGMENTS, D, D), D ** -0.5, 0.09375, ((0, 64), (1, 4), (2, 4)))
    layer_gains = jnp.clip(jax.random.uniform(arg_keys[1], (SEGMENTS, D), jnp.float32, -0.5, 0.5) * block_scale(arg_keys[1], (SEGMENTS, D), ((0, 64), (1, 4)), -0.4, 0.0), -0.5, 0.5)
    incoming = scatter_about(arg_keys[2], (SEGMENTS, TOKENS_MB, D), 1.0, 6.0, ((0, 64), (1, 4), (2, 4)))
    fresh_batch = scatter_about(arg_keys[3], (TOKENS_MB, D), 1.0, 6.0, ((0, 4), (1, 4)))
    returning = scatter_about(arg_keys[4], (SEGMENTS, TOKENS_MB, D), 1.0, 6.0, ((0, 64), (1, 4), (2, 4)))
    fresh_cotangent = scatter_about(arg_keys[5], (TOKENS_MB, D), 1.0, 6.0, ((0, 4), (1, 4)))
    stashed_inputs = scatter_about(arg_keys[6], (SEGMENTS, 2, TOKENS_MB, D), 1.0, 6.0, ((0, 64), (2, 4), (3, 4)))
    return {"weights": weights, "layer_gains": layer_gains, "incoming": incoming, "fresh_batch": fresh_batch, "returning": returning, "fresh_cotangent": fresh_cotangent, "stashed_inputs": stashed_inputs}


def silu_slope(values):
    sigma = jax.nn.sigmoid(values)
    return sigma * (1.0 + values * (1.0 - sigma))


def advance_layer(packed):
    inputs, weight, layer_gain = packed
    pre_act = jnp.dot(inputs, weight, preferred_element_type=jnp.float32)
    return (inputs.astype(jnp.float32) + layer_gain * jax.nn.silu(pre_act)).astype(jnp.bfloat16)


def retreat_layer(packed):
    upstream, stored, weight, layer_gain = packed
    pre_act = jnp.dot(stored, weight, preferred_element_type=jnp.float32)
    scaled = (upstream.astype(jnp.float32) * layer_gain * silu_slope(pre_act)).astype(jnp.bfloat16)
    back_term = jnp.dot(scaled, weight.T, preferred_element_type=jnp.float32)
    return (upstream.astype(jnp.float32) + back_term).astype(jnp.bfloat16)


def reference(weights, layer_gains, incoming, fresh_batch, returning, fresh_cotangent, stashed_inputs):
    first_out = lax.map(advance_layer, (incoming, weights, layer_gains))
    feed = jnp.concatenate([fresh_batch[None], first_out[:-1]], axis=0)
    second_out = lax.map(advance_layer, (feed, weights, layer_gains))
    grad_first = lax.map(retreat_layer, (returning, stashed_inputs[:, 0], weights, layer_gains))
    upstream = jnp.concatenate([grad_first[1:], fresh_cotangent[None]], axis=0)
    grad_second = lax.map(retreat_layer, (upstream, stashed_inputs[:, 1], weights, layer_gains))
    layer_outputs = jnp.stack([first_out, second_out], axis=1)
    input_grads = jnp.stack([grad_first, grad_second], axis=1)
    return layer_outputs, input_grads
```

```python
import functools

import jax
import jax.numpy as jnp
from jax import lax
from jax.experimental import pallas as pl
from jax.experimental.pallas import tpu as pltpu
from jax.sharding import PartitionSpec as P

MESH = pl.DeviceIdType.MESH
BF16 = jnp.bfloat16
F32 = jnp.float32

BACK1, FWD1, BACK2, FWD2 = range(4)
GATHER, CORE, CROSS, RELAY, HOP_UP, HOP_DOWN, LATE_UP, LATE_DOWN, SUM_UP, SUM_DOWN = range(10)
OWN_UP, OWN_DOWN, REST_UP, REST_DOWN, NEXT_UP, NEXT_DOWN, PART_FAR, PART_NEAR, PAIR, HOME = range(10)
STREAM_COPIES = 10
SEG_OUT, SEG_GRAD = 60, 61
COPIES = 62


def token_of(row, col):
    first = jnp.where(col == 0, 0, jnp.where(col == 1, 3, col - 1))
    last = jnp.where(col == 2, 0, jnp.where(col == 3, 3, col + 1))
    return jnp.where(row == 0, first, jnp.where(row == 3, last, col))


def collector_of(row, token):
    first = jnp.where(token == 0, 0, jnp.where(token == 3, 1, token + 1))
    last = jnp.where(token == 0, 2, jnp.where(token == 3, 3, token - 1))
    return jnp.where(row == 0, first, jnp.where(row == 3, last, token))


def kernel(
    segments,
    gain_ref,
    weight_hbm,
    incoming_hbm,
    fresh_hbm,
    returning_hbm,
    cotangent_hbm,
    stash_hbm,
    outputs_hbm,
    grads_hbm,
    weight,
    incoming,
    fresh,
    returning,
    cotangent,
    full_in,
    partial,
    hop_in,
    hop_out,
    last_in,
    scaled,
    back_partial,
    core_in,
    pair_out,
    pair_in,
    home_out,
    home_in,
    result,
    message,
    feed,
    upstream,
    grad,
    grad_message,
    send_sem,
    recv_sem,
    local_sem,
):
    seg = lax.axis_index("segment")
    row = lax.axis_index("row")
    col = lax.axis_index("col")
    block = incoming.shape[0]
    half = block // 2
    width = incoming.shape[1]
    tile = min(256, width)

    up, down, over = (row + 1) % 4, (row + 3) % 4, (row + 2) % 4
    core = col + 1 - 2 * (col % 2)
    cross = (col + 2) % 4
    both = (core + 2) % 4
    token, token_core, token_cross, token_both = [token_of(row, c) for c in (col, core, cross, both)]
    spot = collector_of(col, row)
    seg_next = (seg + 1) % segments
    seg_prev = (seg + segments - 1) % segments
    diagonal = row == col

    dev_core, dev_cross = (seg, row, core), (seg, row, cross)
    dev_up, dev_down = (seg, up, col), (seg, down, col)
    dev_spot, dev_home = (seg, col, spot), (seg, token, row)

    def rows(ref, index, start=0, size=None):
        size = block if size is None else size
        return ref.at[pl.ds(pl.multiple_of(index * block + start, half), size)]

    def send(key, src, dst, device):
        copy = pltpu.make_async_remote_copy(
            src_ref=src,
            dst_ref=dst,
            send_sem=send_sem.at[key],
            recv_sem=recv_sem.at[key],
            device_id=device,
            device_id_type=MESH,
        )
        copy.start()

    def arrived(key, ref):
        pltpu.make_async_remote_copy(
            src_ref=ref,
            dst_ref=ref,
            send_sem=send_sem.at[key],
            recv_sem=recv_sem.at[key],
            device_id=dev_core,
            device_id_type=MESH,
        ).wait_recv()

    def left(key, ref):
        pltpu.make_async_remote_copy(
            src_ref=ref,
            dst_ref=ref,
            send_sem=send_sem.at[key],
            recv_sem=recv_sem.at[key],
            device_id=dev_core,
            device_id_type=MESH,
        ).wait_send()

    loads = [
        pltpu.make_async_copy(src, dst, local_sem.at[at])
        for at, (src, dst) in enumerate(
            [
                (weight_hbm, weight),
                (incoming_hbm, incoming),
                (returning_hbm, returning),
                (fresh_hbm, fresh),
                (cotangent_hbm, cotangent),
            ]
        )
    ]
    for load in loads:
        load.start()

    barrier = pltpu.get_barrier_semaphore()
    others = [
        dev_core,
        dev_cross,
        dev_up,
        dev_down,
        (seg_next, row, col),
        (seg_prev, row, col),
        (seg_next, col, spot),
        (seg_prev, token, row),
    ]
    for device in others:
        pl.semaphore_signal(barrier, inc=1, device_id=device, device_id_type=MESH)

    @pl.when(diagonal)
    def _():
        pl.semaphore_wait(barrier, len(others))

    @pl.when(jnp.logical_not(diagonal))
    def _():
        for device in (dev_spot, dev_home):
            pl.semaphore_signal(barrier, inc=1, device_id=device, device_id_type=MESH)
        pl.semaphore_wait(barrier, len(others) + 2)

    def key_of(stream, step):
        return stream * STREAM_COPIES + step

    def back_key(tick, step):
        return (4 + tick) * STREAM_COPIES + step

    def gather(stream, source):
        key = key_of(stream, GATHER)
        target = rows(full_in.at[stream], row)

        @pl.when(diagonal)
        def _():
            pltpu.make_async_copy(source, target, recv_sem.at[key]).start()

        @pl.when(jnp.logical_not(diagonal))
        def _():
            send(key, source, target, dev_spot)

    def share(stream):
        mine = rows(full_in.at[stream], token)
        arrived(key_of(stream, GATHER), mine)
        send(key_of(stream, CROSS), mine, mine, dev_cross)
        send(key_of(stream, CORE), mine, mine, dev_core)

    def relay(stream):
        theirs = rows(full_in.at[stream], token_cross)
        arrived(key_of(stream, CROSS), theirs)
        send(key_of(stream, RELAY), theirs, theirs, dev_core)

    def multiply(stream):
        arrived(key_of(stream, CORE), rows(full_in.at[stream], token_core))
        arrived(key_of(stream, RELAY), rows(full_in.at[stream], token_both))

        @pl.loop(0, width // tile)
        def _(step):
            at = pl.ds(pl.multiple_of(step * tile, tile), tile)
            partial[stream, :, at] = jnp.dot(
                full_in[stream], weight[:, at], preferred_element_type=F32
            ).astype(BF16)

        mine, reach, final = partial.at[stream], hop_in.at[stream], last_in.at[stream]
        send(key_of(stream, HOP_UP), rows(mine, over, 0, half), reach.at[0], dev_up)
        send(key_of(stream, HOP_DOWN), rows(mine, over, half, half), reach.at[1], dev_down)
        send(key_of(stream, LATE_UP), rows(mine, up, half, half), final.at[0, pl.ds(half, half)], dev_up)
        send(key_of(stream, LATE_DOWN), rows(mine, down, 0, half), final.at[1, pl.ds(0, half)], dev_down)

    def pass_sum(stream):
        mine, reach, final = partial.at[stream], hop_in.at[stream], last_in.at[stream]
        arrived(key_of(stream, HOP_UP), reach.at[0])
        hop_out[stream, 0] = (reach[0].astype(F32) + rows(mine, up, 0, half)[...].astype(F32)).astype(BF16)
        send(key_of(stream, SUM_UP), hop_out.at[stream, 0], final.at[0, pl.ds(0, half)], dev_up)
        arrived(key_of(stream, HOP_DOWN), reach.at[1])
        hop_out[stream, 1] = (reach[1].astype(F32) + rows(mine, down, half, half)[...].astype(F32)).astype(BF16)
        send(key_of(stream, SUM_DOWN), hop_out.at[stream, 1], final.at[1, pl.ds(half, half)], dev_down)

    def pre_activation(stream):
        final = last_in.at[stream]
        arrived(key_of(stream, LATE_UP), final.at[0, pl.ds(half, half)])
        arrived(key_of(stream, LATE_DOWN), final.at[1, pl.ds(0, half)])
        arrived(key_of(stream, SUM_UP), final.at[0, pl.ds(0, half)])
        arrived(key_of(stream, SUM_DOWN), final.at[1, pl.ds(half, half)])
        own = rows(partial.at[stream], row)[...].astype(F32)
        return own + final[0].astype(F32) + final[1].astype(F32)

    def advance(stream, own_block):
        pre = pre_activation(stream)
        return (own_block.astype(F32) + gain_ref[...] * (pre * jax.nn.sigmoid(pre))).astype(BF16)

    def scale(tick, stream, coming):
        pre = pre_activation(stream)
        sigma = jax.nn.sigmoid(pre)
        slope = sigma * (1.0 + pre * (1.0 - sigma))
        all_rows = scaled.at[tick]
        rows(all_rows, row)[...] = (coming.astype(F32) * gain_ref[...] * slope).astype(BF16)
        low, high = rows(all_rows, row, 0, half), rows(all_rows, row, half, half)
        send(back_key(tick, OWN_UP), low, low, dev_up)
        send(back_key(tick, OWN_DOWN), high, high, dev_down)
        send(back_key(tick, REST_UP), high, high, dev_up)
        send(back_key(tick, REST_DOWN), low, low, dev_down)

    def pass_scaled(tick):
        low, high = rows(scaled.at[tick], down, 0, half), rows(scaled.at[tick], up, half, half)
        arrived(back_key(tick, OWN_UP), low)
        send(back_key(tick, NEXT_UP), low, low, dev_up)
        arrived(back_key(tick, OWN_DOWN), high)
        send(back_key(tick, NEXT_DOWN), high, high, dev_down)

    def multiply_back(tick):
        all_rows = scaled.at[tick]
        arrived(back_key(tick, REST_UP), rows(all_rows, down, half, half))
        arrived(back_key(tick, REST_DOWN), rows(all_rows, up, 0, half))
        arrived(back_key(tick, NEXT_UP), rows(all_rows, over, 0, half))
        arrived(back_key(tick, NEXT_DOWN), rows(all_rows, over, half, half))

        @pl.loop(0, width // tile)
        def _(step):
            at = pl.ds(pl.multiple_of(step * tile, tile), tile)
            back_partial[tick, :, at] = lax.dot_general(
                scaled[tick], weight[at, :], (((1,), (1,)), ((), ())), preferred_element_type=F32
            ).astype(BF16)

        mine = back_partial.at[tick]
        send(back_key(tick, PART_FAR), rows(mine, token_both), core_in.at[tick, 1], dev_core)
        send(back_key(tick, PART_NEAR), rows(mine, token_core), core_in.at[tick, 0], dev_core)

    def pair_sum(tick):
        arrived(back_key(tick, PART_FAR), core_in.at[tick, 1])
        own = rows(back_partial.at[tick], token_cross)[...].astype(F32)
        pair_out[tick] = (own + core_in[tick, 1].astype(F32)).astype(BF16)
        send(back_key(tick, PAIR), pair_out.at[tick], pair_in.at[tick], dev_cross)

    def home_sum(tick):
        arrived(back_key(tick, PART_NEAR), core_in.at[tick, 0])
        arrived(back_key(tick, PAIR), pair_in.at[tick])
        own = rows(back_partial.at[tick], token)[...].astype(F32)
        home_out[tick] = (own + core_in[tick, 0].astype(F32) + pair_in[tick].astype(F32)).astype(BF16)
        key = back_key(tick, HOME)

        @pl.when(diagonal)
        def _():
            pltpu.make_async_copy(home_out.at[tick], home_in.at[tick], recv_sem.at[key]).start()

        @pl.when(jnp.logical_not(diagonal))
        def _():
            send(key, home_out.at[tick], home_in.at[tick], dev_home)

    def gradient(tick, coming):
        arrived(back_key(tick, HOME), home_in.at[tick])
        return (coming.astype(F32) + home_in[tick].astype(F32)).astype(BF16)

    def store(at, src, dst):
        copy = pltpu.make_async_copy(src, dst, local_sem.at[at])
        copy.start()
        return copy

    gather(BACK1, stash_hbm.at[0])
    gather(FWD1, incoming_hbm)
    gather(BACK2, stash_hbm.at[1])
    share(BACK1)
    share(FWD1)
    relay(BACK1)
    for load in loads:
        load.wait()
    relay(FWD1)
    multiply(BACK1)
    multiply(FWD1)
    share(BACK2)
    pass_sum(BACK1)
    relay(BACK2)
    pass_sum(FWD1)
    scale(0, BACK1, returning[...])
    result[0] = advance(FWD1, incoming[...])
    message[...] = jnp.where(seg == segments - 1, fresh[...], result[0])
    send(SEG_OUT, message, feed, (seg_next, row, col))
    send(key_of(FWD2, GATHER), message, rows(full_in.at[FWD2], row), (seg_next, col, spot))
    multiply(BACK2)
    pass_scaled(0)
    stores = [store(5, result.at[0], outputs_hbm.at[0])]
    share(FWD2)
    pass_sum(BACK2)
    multiply_back(0)
    pair_sum(0)
    relay(FWD2)
    home_sum(0)
    multiply(FWD2)
    grad[0] = gradient(0, returning[...])
    grad_message[...] = jnp.where(seg == 0, cotangent[...], grad[0])
    send(SEG_GRAD, grad_message, upstream, (seg_prev, row, col))
    stores.append(store(6, grad.at[0], grads_hbm.at[0]))
    arrived(SEG_GRAD, upstream)
    scale(1, BACK2, upstream[...])
    pass_sum(FWD2)
    pass_scaled(1)
    arrived(SEG_OUT, feed)
    result[1] = advance(FWD2, feed[...])
    stores.append(store(7, result.at[1], outputs_hbm.at[1]))
    multiply_back(1)
    pair_sum(1)
    home_sum(1)
    grad[1] = gradient(1, upstream[...])
    stores.append(store(8, grad.at[1], grads_hbm.at[1]))

    for stream in range(4):
        whole = rows(full_in.at[stream], row)
        if stream != FWD2:

            @pl.when(jnp.logical_not(diagonal))
            def _():
                left(key_of(stream, GATHER), whole)
        else:
            left(key_of(stream, GATHER), whole)
        for step in (CORE, CROSS, RELAY):
            left(key_of(stream, step), whole)
        for step in (HOP_UP, HOP_DOWN, LATE_UP, LATE_DOWN, SUM_UP, SUM_DOWN):
            left(key_of(stream, step), hop_in.at[stream, 0])
    for tick in range(2):
        for step in (OWN_UP, OWN_DOWN, REST_UP, REST_DOWN, NEXT_UP, NEXT_DOWN):
            left(back_key(tick, step), hop_in.at[0, 0])
        for step in (PART_FAR, PART_NEAR, PAIR):
            left(back_key(tick, step), pair_in.at[tick])

        @pl.when(jnp.logical_not(diagonal))
        def _():
            left(back_key(tick, HOME), home_in.at[tick])

    left(SEG_OUT, feed)
    left(SEG_GRAD, upstream)
    for copy in stores:
        copy.wait()


def relay_call(segments, weights, gains, incoming, fresh, returning, cotangent, stashed):
    block, width = incoming.shape
    half, tokens = block // 2, 4 * block
    piece = (block, width)
    hbm = pl.BlockSpec(memory_space=pl.ANY)
    vmem = lambda *shape: pltpu.VMEM(shape, BF16)
    return pl.pallas_call(
        functools.partial(kernel, segments),
        out_shape=[jax.ShapeDtypeStruct((2,) + piece, BF16)] * 2,
        in_specs=[pl.BlockSpec(memory_space=pltpu.VMEM)] + [hbm] * 6,
        out_specs=[hbm] * 2,
        scratch_shapes=[
            vmem(width, width),
            vmem(*piece),
            vmem(*piece),
            vmem(*piece),
            vmem(*piece),
            vmem(4, tokens, width),
            vmem(4, tokens, width),
            vmem(4, 2, half, width),
            vmem(4, 2, half, width),
            vmem(4, 2, block, width),
            vmem(2, tokens, width),
            vmem(2, tokens, width),
            vmem(2, 2, block, width),
            vmem(2, block, width),
            vmem(2, block, width),
            vmem(2, block, width),
            vmem(2, block, width),
            vmem(2, block, width),
            vmem(*piece),
            vmem(*piece),
            vmem(*piece),
            vmem(2, block, width),
            vmem(*piece),
            pltpu.SemaphoreType.DMA((COPIES,)),
            pltpu.SemaphoreType.DMA((COPIES,)),
            pltpu.SemaphoreType.DMA((9,)),
        ],
        compiler_params=pltpu.CompilerParams(collective_id=0, has_side_effects=True),
    )(gains, weights, incoming, fresh, returning, cotangent, stashed)


def solution(mesh):
    segments = mesh.shape["segment"]

    def shards(weights, layer_gains, incoming, fresh_batch, returning, fresh_cotangent, stashed_inputs):
        outputs, grads = relay_call(
            segments,
            weights[0],
            layer_gains,
            incoming[0],
            fresh_batch,
            returning[0],
            fresh_cotangent,
            stashed_inputs[0],
        )
        return outputs[None], grads[None]

    in_specs = (
        P("segment", "row", "col"),
        P("segment", "col"),
        P("segment", "row", "col"),
        P("row", "col"),
        P("segment", "row", "col"),
        P("row", "col"),
        P("segment", None, "row", "col"),
    )
    out_specs = (P("segment", None, "row", "col"), P("segment", None, "row", "col"))
    return jax.shard_map(shards, mesh=mesh, in_specs=in_specs, out_specs=out_specs, check_vma=False)
```

```python
import functools

import jax
import jax.numpy as jnp
from jax import lax
from jax.experimental import pallas as pl
from jax.experimental.pallas import tpu as pltpu
from jax.sharding import PartitionSpec as P

MESH = pl.DeviceIdType.MESH
BF16 = jnp.bfloat16
F32 = jnp.float32

BACK1, FWD1, BACK2, FWD2 = range(4)
GATHER, CROSS, RELAY, CORE, HOP_UP, HOP_DOWN, LATE_UP, LATE_DOWN, SUM_UP, SUM_DOWN = 0, 2, 4, 6, 7, 8, 9, 10, 11, 12
STREAM_COPIES = 13
OWN_UP, OWN_DOWN, REST_UP, REST_DOWN, NEXT_UP, NEXT_DOWN, PART_NEAR, PART_FAR, PAIR, HOME = 0, 1, 2, 3, 4, 5, 6, 7, 9, 11
BACK_COPIES = 13
BACK_START = 4 * STREAM_COPIES
SEG_OUT = BACK_START + 2 * BACK_COPIES
SEG_RETURNING, SEG_TERM = SEG_OUT + 1, SEG_OUT + 2
COPIES = SEG_OUT + 3


def token_of(row, col):
    first = jnp.where(col == 0, 0, jnp.where(col == 1, 3, col - 1))
    last = jnp.where(col == 2, 0, jnp.where(col == 3, 3, col + 1))
    return jnp.where(row == 0, first, jnp.where(row == 3, last, col))


def collector_of(row, token):
    first = jnp.where(token == 0, 0, jnp.where(token == 3, 1, token + 1))
    last = jnp.where(token == 0, 2, jnp.where(token == 3, 3, token - 1))
    return jnp.where(row == 0, first, jnp.where(row == 3, last, token))


def kernel(
    segments,
    gain_ref,
    weight_hbm,
    incoming_hbm,
    fresh_hbm,
    returning_hbm,
    cotangent_hbm,
    stash_hbm,
    outputs_hbm,
    grads_hbm,
    weight,
    incoming,
    fresh,
    returning,
    cotangent,
    full_in,
    partial,
    hop_in,
    hop_out,
    last_in,
    scaled,
    back_partial,
    core_in,
    pair_out,
    pair_in,
    home_out,
    home_in,
    result,
    message,
    feed,
    upstream,
    grad,
    returning_next,
    term,
    send_sem,
    recv_sem,
    local_sem,
    here_sem,
):
    seg = lax.axis_index("segment")
    row = lax.axis_index("row")
    col = lax.axis_index("col")
    block = incoming.shape[0]
    half = block // 2
    width = incoming.shape[1]
    tile = min(256, width)

    up, down, over = (row + 1) % 4, (row + 3) % 4, (row + 2) % 4
    core = col + 1 - 2 * (col % 2)
    cross = (col + 2) % 4
    both = (core + 2) % 4
    token, token_core, token_cross, token_both = [token_of(row, c) for c in (col, core, cross, both)]
    spot = collector_of(col, row)
    seg_next = (seg + 1) % segments
    seg_prev = (seg + segments - 1) % segments
    diagonal = row == col

    dev_core, dev_cross = (seg, row, core), (seg, row, cross)
    dev_up, dev_down = (seg, up, col), (seg, down, col)
    dev_spot, dev_home = (seg, col, spot), (seg, token, row)

    def rows(ref, index, start=0, size=None):
        size = block if size is None else size
        return ref.at[pl.ds(pl.multiple_of(index * block + start, half), size)]

    sent = {}

    def send(key, src, dst, device):
        sent[key] = dst.shape[0] == half
        copy = pltpu.make_async_remote_copy(
            src_ref=src,
            dst_ref=dst,
            send_sem=send_sem.at[key],
            recv_sem=recv_sem.at[key],
            device_id=device,
            device_id_type=MESH,
        )
        copy.start()

    def arrived(key, ref):
        pltpu.make_async_remote_copy(
            src_ref=ref,
            dst_ref=ref,
            send_sem=send_sem.at[key],
            recv_sem=recv_sem.at[key],
            device_id=dev_core,
            device_id_type=MESH,
        ).wait_recv()

    def left(key, ref):
        pltpu.make_async_remote_copy(
            src_ref=ref,
            dst_ref=ref,
            send_sem=send_sem.at[key],
            recv_sem=recv_sem.at[key],
            device_id=dev_core,
            device_id_type=MESH,
        ).wait_send()

    loads = [
        pltpu.make_async_copy(src, dst, local_sem.at[at])
        for at, (src, dst) in enumerate(
            [
                (weight_hbm, weight),
                (incoming_hbm, incoming),
                (returning_hbm, returning),
                (fresh_hbm, fresh),
                (cotangent_hbm, cotangent),
            ]
        )
    ]
    for load in loads:
        load.start()

    barrier = pltpu.get_barrier_semaphore()
    others = [dev_core, dev_cross, dev_up, dev_down, (seg_prev, row, col), (seg_prev, token, row)]
    for device in others:
        pl.semaphore_signal(barrier, inc=1, device_id=device, device_id_type=MESH)

    @pl.when(diagonal)
    def _():
        pl.semaphore_wait(barrier, len(others))

    @pl.when(jnp.logical_not(diagonal))
    def _():
        for device in (dev_spot, dev_home):
            pl.semaphore_signal(barrier, inc=1, device_id=device, device_id_type=MESH)
        pl.semaphore_wait(barrier, len(others) + 2)

    for device in ((seg_next, row, col), (seg_next, col, spot)):
        pl.semaphore_signal(here_sem, inc=1, device_id=device, device_id_type=MESH)

    def key_of(stream, step):
        return stream * STREAM_COPIES + step

    def back_key(tick, step):
        return BACK_START + tick * BACK_COPIES + step

    def gather(stream, source):
        def pieces():
            for part in range(2):
                piece = source.at[pl.ds(part * half, half)]
                yield key_of(stream, GATHER) + part, piece, rows(full_in.at[stream], row, part * half, half)

        @pl.when(diagonal)
        def _():
            for key, piece, target in pieces():
                pltpu.make_async_copy(piece, target, recv_sem.at[key]).start()

        @pl.when(jnp.logical_not(diagonal))
        def _():
            for key, piece, target in pieces():
                send(key, piece, target, dev_spot)

    def share(stream):
        for part in range(2):
            mine = rows(full_in.at[stream], token, part * half, half)
            arrived(key_of(stream, GATHER) + part, mine)
            send(key_of(stream, CROSS) + part, mine, mine, dev_cross)
        mine = rows(full_in.at[stream], token)
        send(key_of(stream, CORE), mine, mine, dev_core)

    def relay(stream):
        for part in range(2):
            theirs = rows(full_in.at[stream], token_cross, part * half, half)
            arrived(key_of(stream, CROSS) + part, theirs)
            send(key_of(stream, RELAY) + part, theirs, theirs, dev_core)

    def multiply(stream):
        arrived(key_of(stream, CORE), rows(full_in.at[stream], token_core))
        for part in range(2):
            arrived(key_of(stream, RELAY) + part, rows(full_in.at[stream], token_both, part * half, half))

        @pl.loop(0, width // tile)
        def _(step):
            at = pl.ds(pl.multiple_of(step * tile, tile), tile)
            partial[stream, :, at] = jnp.dot(
                full_in[stream], weight[:, at], preferred_element_type=F32
            ).astype(BF16)

        mine, reach, final = partial.at[stream], hop_in.at[stream], last_in.at[stream]
        send(key_of(stream, HOP_UP), rows(mine, over, 0, half), reach.at[0], dev_up)
        send(key_of(stream, HOP_DOWN), rows(mine, over, half, half), reach.at[1], dev_down)
        send(key_of(stream, LATE_UP), rows(mine, up, half, half), final.at[0, pl.ds(half, half)], dev_up)
        send(key_of(stream, LATE_DOWN), rows(mine, down, 0, half), final.at[1, pl.ds(0, half)], dev_down)

    def pass_sum(stream):
        mine, reach, final = partial.at[stream], hop_in.at[stream], last_in.at[stream]
        arrived(key_of(stream, HOP_UP), reach.at[0])
        hop_out[stream, 0] = (reach[0].astype(F32) + rows(mine, up, 0, half)[...].astype(F32)).astype(BF16)
        send(key_of(stream, SUM_UP), hop_out.at[stream, 0], final.at[0, pl.ds(0, half)], dev_up)
        arrived(key_of(stream, HOP_DOWN), reach.at[1])
        hop_out[stream, 1] = (reach[1].astype(F32) + rows(mine, down, half, half)[...].astype(F32)).astype(BF16)
        send(key_of(stream, SUM_DOWN), hop_out.at[stream, 1], final.at[1, pl.ds(half, half)], dev_down)

    def pre_activation(stream):
        final = last_in.at[stream]
        arrived(key_of(stream, LATE_UP), final.at[0, pl.ds(half, half)])
        arrived(key_of(stream, LATE_DOWN), final.at[1, pl.ds(0, half)])
        arrived(key_of(stream, SUM_UP), final.at[0, pl.ds(0, half)])
        arrived(key_of(stream, SUM_DOWN), final.at[1, pl.ds(half, half)])
        own = rows(partial.at[stream], row)[...].astype(F32)
        return own + final[0].astype(F32) + final[1].astype(F32)

    def advance(stream, own_block):
        pre = pre_activation(stream)
        return (own_block.astype(F32) + gain_ref[...] * (pre * jax.nn.sigmoid(pre))).astype(BF16)

    def scale(tick, stream, coming):
        pre = pre_activation(stream)
        sigma = jax.nn.sigmoid(pre)
        slope = sigma * (1.0 + pre * (1.0 - sigma))
        all_rows = scaled.at[tick]
        rows(all_rows, row)[...] = (coming.astype(F32) * gain_ref[...] * slope).astype(BF16)
        low, high = rows(all_rows, row, 0, half), rows(all_rows, row, half, half)
        send(back_key(tick, OWN_UP), low, low, dev_up)
        send(back_key(tick, OWN_DOWN), high, high, dev_down)
        send(back_key(tick, REST_UP), high, high, dev_up)
        send(back_key(tick, REST_DOWN), low, low, dev_down)

    def pass_scaled(tick):
        low, high = rows(scaled.at[tick], down, 0, half), rows(scaled.at[tick], up, half, half)
        arrived(back_key(tick, OWN_UP), low)
        send(back_key(tick, NEXT_UP), low, low, dev_up)
        arrived(back_key(tick, OWN_DOWN), high)
        send(back_key(tick, NEXT_DOWN), high, high, dev_down)

    def multiply_back(tick):
        all_rows = scaled.at[tick]
        arrived(back_key(tick, REST_UP), rows(all_rows, down, half, half))
        arrived(back_key(tick, REST_DOWN), rows(all_rows, up, 0, half))
        arrived(back_key(tick, NEXT_UP), rows(all_rows, over, 0, half))
        arrived(back_key(tick, NEXT_DOWN), rows(all_rows, over, half, half))

        @pl.loop(0, width // tile)
        def _(step):
            at = pl.ds(pl.multiple_of(step * tile, tile), tile)
            back_partial[tick, :, at] = lax.dot_general(
                scaled[tick], weight[at, :], (((1,), (1,)), ((), ())), preferred_element_type=F32
            ).astype(BF16)

        mine = back_partial.at[tick]
        for part in range(2):
            far = core_in.at[tick, 1, pl.ds(part * half, half)]
            send(back_key(tick, PART_FAR) + part, rows(mine, token_both, part * half, half), far, dev_core)
        send(back_key(tick, PART_NEAR), rows(mine, token_core), core_in.at[tick, 0], dev_core)

    def pair_sum(tick):
        for part in range(2):
            at = pl.ds(part * half, half)
            arrived(back_key(tick, PART_FAR) + part, core_in.at[tick, 1, at])
            own = rows(back_partial.at[tick], token_cross, part * half, half)[...].astype(F32)
            pair_out[tick, at] = (own + core_in[tick, 1, at].astype(F32)).astype(BF16)
            send(back_key(tick, PAIR) + part, pair_out.at[tick, at], pair_in.at[tick, at], dev_cross)

    def home_sum(tick):
        arrived(back_key(tick, PART_NEAR), core_in.at[tick, 0])
        for part in range(2):
            at = pl.ds(part * half, half)
            key = back_key(tick, HOME) + part
            arrived(back_key(tick, PAIR) + part, pair_in.at[tick, at])
            own = rows(back_partial.at[tick], token, part * half, half)[...].astype(F32)
            home_out[tick, at] = (own + core_in[tick, 0, at].astype(F32) + pair_in[tick, at].astype(F32)).astype(BF16)
            if tick == 0:
                send(key, home_out.at[tick, at], home_in.at[tick, at], (seg_prev, token, row))
                continue

            @pl.when(diagonal)
            def _():
                pltpu.make_async_copy(home_out.at[tick, at], home_in.at[tick, at], recv_sem.at[key]).start()

            @pl.when(jnp.logical_not(diagonal))
            def _():
                send(key, home_out.at[tick, at], home_in.at[tick, at], dev_home)

    def home_arrived(tick):
        for part in range(2):
            arrived(back_key(tick, HOME) + part, home_in.at[tick, pl.ds(part * half, half)])

    def added(coming, term):
        return (coming.astype(F32) + term.astype(F32)).astype(BF16)

    def store(at, src, dst):
        copy = pltpu.make_async_copy(src, dst, local_sem.at[at])
        copy.start()
        return copy

    def wait_loads():
        for load in loads:
            load.wait()

    stores = []

    def pass_on_output():
        result[0] = advance(FWD1, incoming[...])
        message[...] = jnp.where(seg == segments - 1, fresh[...], result[0])
        send(key_of(FWD2, GATHER), message.at[pl.ds(0, half)], rows(full_in.at[FWD2], row, 0, half), (seg_next, col, spot))
        send(key_of(FWD2, GATHER) + 1, message.at[pl.ds(half, half)], rows(full_in.at[FWD2], row, half, half), (seg_next, col, spot))
        send(SEG_OUT, message, feed, (seg_next, row, col))
        stores.append(store(5, result.at[0], outputs_hbm.at[0]))

    def pass_on_returning():
        pl.semaphore_wait(here_sem, 2)
        send(SEG_RETURNING, returning_hbm, returning_next, (seg_prev, row, col))

    def scale_second():
        arrived(SEG_RETURNING, returning_next)
        home_arrived(0)
        following = added(returning_next[...], home_in[0])
        upstream[...] = jnp.where(seg == segments - 1, cotangent[...], following)
        scale(1, BACK2, upstream[...])
        send(SEG_TERM, home_in.at[0], term, (seg_next, row, col))

    def finish_first():
        arrived(SEG_TERM, term)
        grad[0] = added(returning[...], term[...])
        stores.append(store(6, grad.at[0], grads_hbm.at[0]))

    def finish_output():
        arrived(SEG_OUT, feed)
        result[1] = advance(FWD2, feed[...])
        stores.append(store(7, result.at[1], outputs_hbm.at[1]))

    def finish_gradient():
        home_arrived(1)
        grad[1] = added(upstream[...], home_in[1])
        stores.append(store(8, grad.at[1], grads_hbm.at[1]))

    gather(BACK1, stash_hbm.at[0])
    gather(FWD1, incoming_hbm)
    share(BACK1)
    gather(BACK2, stash_hbm.at[1])
    share(FWD1)
    relay(BACK1)
    wait_loads()
    multiply(BACK1)
    relay(FWD1)
    share(BACK2)
    multiply(FWD1)
    relay(BACK2)
    pass_sum(BACK1)
    pass_sum(FWD1)
    scale(0, BACK1, returning[...])
    multiply(BACK2)
    pass_on_returning()
    pass_on_output()
    pass_scaled(0)
    pass_sum(BACK2)
    multiply_back(0)
    pair_sum(0)
    home_sum(0)
    share(FWD2)
    scale_second()
    relay(FWD2)
    multiply(FWD2)
    pass_scaled(1)
    pass_sum(FWD2)
    multiply_back(1)
    finish_first()
    pair_sum(1)
    home_sum(1)
    finish_output()
    finish_gradient()

    around = [key_of(stream, GATHER) + part for stream in (BACK1, FWD1, BACK2) for part in range(2)]
    around += [back_key(1, HOME) + part for part in range(2)]
    for key, is_half in sent.items():
        if key not in around:
            left(key, hop_in.at[0, 0] if is_half else home_in.at[0])

    @pl.when(jnp.logical_not(diagonal))
    def _():
        for key in around:
            left(key, hop_in.at[0, 0])

    for copy in stores:
        copy.wait()


def relay_call(segments, weights, gains, incoming, fresh, returning, cotangent, stashed):
    block, width = incoming.shape
    half, tokens = block // 2, 4 * block
    piece = (block, width)
    hbm = pl.BlockSpec(memory_space=pl.ANY)
    vmem = lambda *shape: pltpu.VMEM(shape, BF16)
    return pl.pallas_call(
        functools.partial(kernel, segments),
        out_shape=[jax.ShapeDtypeStruct((2,) + piece, BF16)] * 2,
        in_specs=[pl.BlockSpec(memory_space=pltpu.VMEM)] + [hbm] * 6,
        out_specs=[hbm] * 2,
        scratch_shapes=[
            vmem(width, width),
            vmem(*piece),
            vmem(*piece),
            vmem(*piece),
            vmem(*piece),
            vmem(4, tokens, width),
            vmem(4, tokens, width),
            vmem(4, 2, half, width),
            vmem(4, 2, half, width),
            vmem(4, 2, block, width),
            vmem(2, tokens, width),
            vmem(2, tokens, width),
            vmem(2, 2, block, width),
            vmem(2, block, width),
            vmem(2, block, width),
            vmem(2, block, width),
            vmem(2, block, width),
            vmem(2, block, width),
            vmem(*piece),
            vmem(*piece),
            vmem(*piece),
            vmem(2, block, width),
            vmem(*piece),
            vmem(*piece),
            pltpu.SemaphoreType.DMA((COPIES,)),
            pltpu.SemaphoreType.DMA((COPIES,)),
            pltpu.SemaphoreType.DMA((9,)),
            pltpu.SemaphoreType.REGULAR,
        ],
        compiler_params=pltpu.CompilerParams(collective_id=0, has_side_effects=True),
    )(gains, weights, incoming, fresh, returning, cotangent, stashed)


def solution(mesh):
    segments = mesh.shape["segment"]

    def shards(weights, layer_gains, incoming, fresh_batch, returning, fresh_cotangent, stashed_inputs):
        outputs, grads = relay_call(
            segments,
            weights[0],
            layer_gains,
            incoming[0],
            fresh_batch,
            returning[0],
            fresh_cotangent,
            stashed_inputs[0],
        )
        return outputs[None], grads[None]

    in_specs = (
        P("segment", "row", "col"),
        P("segment", "col"),
        P("segment", "row", "col"),
        P("row", "col"),
        P("segment", "row", "col"),
        P("row", "col"),
        P("segment", None, "row", "col"),
    )
    out_specs = (P("segment", None, "row", "col"), P("segment", None, "row", "col"))
    return jax.shard_map(shards, mesh=mesh, in_specs=in_specs, out_specs=out_specs, check_vma=False)
```

```python
import functools

import jax
import jax.numpy as jnp
from jax import lax
from jax.experimental import pallas as pl
from jax.experimental.pallas import tpu as pltpu
from jax.sharding import PartitionSpec as P

MESH = pl.DeviceIdType.MESH
BF16 = jnp.bfloat16
F32 = jnp.float32

BACK1, FWD1, BACK2, FWD2 = range(4)
GATHER, CROSS, RELAY, CORE, HOP_UP, HOP_DOWN, LATE_UP, LATE_DOWN, SUM_UP, SUM_DOWN = 0, 2, 4, 6, 7, 8, 9, 10, 11, 12
STREAM_COPIES = 13
OWN_UP, OWN_DOWN, REST_UP, REST_DOWN, NEXT_UP, NEXT_DOWN, PART_NEAR, PART_FAR, PAIR, HOME = 0, 1, 2, 3, 4, 5, 6, 7, 9, 11
BACK_COPIES = 13
BACK_START = 4 * STREAM_COPIES
SEG_OUT = BACK_START + 2 * BACK_COPIES
SEG_RETURNING, SEG_TERM = SEG_OUT + 1, SEG_OUT + 2
COPIES = SEG_OUT + 3


def token_of(row, col):
    first = jnp.where(col == 0, 0, jnp.where(col == 1, 3, col - 1))
    last = jnp.where(col == 2, 0, jnp.where(col == 3, 3, col + 1))
    return jnp.where(row == 0, first, jnp.where(row == 3, last, col))


def collector_of(row, token):
    first = jnp.where(token == 0, 0, jnp.where(token == 3, 1, token + 1))
    last = jnp.where(token == 0, 2, jnp.where(token == 3, 3, token - 1))
    return jnp.where(row == 0, first, jnp.where(row == 3, last, token))


def kernel(
    segments,
    gain_ref,
    weight_hbm,
    incoming_hbm,
    fresh_hbm,
    returning_hbm,
    cotangent_hbm,
    stash_hbm,
    both_hbm,
    weight,
    incoming,
    fresh,
    returning,
    cotangent,
    full_in,
    partial,
    hop_in,
    hop_out,
    last_in,
    scaled,
    back_partial,
    core_in,
    pair_out,
    pair_in,
    home_out,
    home_in,
    result,
    message,
    feed,
    upstream,
    grad,
    returning_next,
    term,
    send_sem,
    recv_sem,
    local_sem,
    here_sem,
):
    seg = lax.axis_index("segment")
    row = lax.axis_index("row")
    col = lax.axis_index("col")
    block = incoming.shape[0]
    half = block // 2
    width = incoming.shape[1]
    tile = min(256, width)

    up, down, over = (row + 1) % 4, (row + 3) % 4, (row + 2) % 4
    core = col + 1 - 2 * (col % 2)
    cross = (col + 2) % 4
    both = (core + 2) % 4
    token, token_core, token_cross, token_both = [token_of(row, c) for c in (col, core, cross, both)]
    spot = collector_of(col, row)
    seg_next = (seg + 1) % segments
    seg_prev = (seg + segments - 1) % segments
    diagonal = row == col

    dev_core, dev_cross = (seg, row, core), (seg, row, cross)
    dev_up, dev_down = (seg, up, col), (seg, down, col)
    dev_spot, dev_home = (seg, col, spot), (seg, token, row)

    def rows(ref, index, start=0, size=None):
        size = block if size is None else size
        return ref.at[pl.ds(pl.multiple_of(index * block + start, half), size)]

    sent = {}

    def send(key, src, dst, device):
        sent[key] = dst.shape[0] == half
        copy = pltpu.make_async_remote_copy(
            src_ref=src,
            dst_ref=dst,
            send_sem=send_sem.at[key],
            recv_sem=recv_sem.at[key],
            device_id=device,
            device_id_type=MESH,
        )
        copy.start()

    def arrived(key, ref):
        pltpu.make_async_remote_copy(
            src_ref=ref,
            dst_ref=ref,
            send_sem=send_sem.at[key],
            recv_sem=recv_sem.at[key],
            device_id=dev_core,
            device_id_type=MESH,
        ).wait_recv()

    def left(key, ref):
        pltpu.make_async_remote_copy(
            src_ref=ref,
            dst_ref=ref,
            send_sem=send_sem.at[key],
            recv_sem=recv_sem.at[key],
            device_id=dev_core,
            device_id_type=MESH,
        ).wait_send()

    loads = [
        pltpu.make_async_copy(src, dst, local_sem.at[at])
        for at, (src, dst) in enumerate(
            [
                (weight_hbm, weight),
                (incoming_hbm, incoming),
                (returning_hbm, returning),
                (fresh_hbm, fresh),
                (cotangent_hbm, cotangent),
            ]
        )
    ]
    for load in loads:
        load.start()

    barrier = pltpu.get_barrier_semaphore()
    others = [dev_core, dev_cross, dev_up, dev_down, (seg_prev, row, col), (seg_prev, token, row)]
    for device in others:
        pl.semaphore_signal(barrier, inc=1, device_id=device, device_id_type=MESH)

    @pl.when(diagonal)
    def _():
        pl.semaphore_wait(barrier, len(others))

    @pl.when(jnp.logical_not(diagonal))
    def _():
        for device in (dev_spot, dev_home):
            pl.semaphore_signal(barrier, inc=1, device_id=device, device_id_type=MESH)
        pl.semaphore_wait(barrier, len(others) + 2)

    for device in ((seg_next, row, col), (seg_next, col, spot)):
        pl.semaphore_signal(here_sem, inc=1, device_id=device, device_id_type=MESH)

    def key_of(stream, step):
        return stream * STREAM_COPIES + step

    def back_key(tick, step):
        return BACK_START + tick * BACK_COPIES + step

    def gather(stream, source):
        def pieces():
            for part in range(2):
                piece = source.at[pl.ds(part * half, half)]
                yield key_of(stream, GATHER) + part, piece, rows(full_in.at[stream], row, part * half, half)

        @pl.when(diagonal)
        def _():
            for key, piece, target in pieces():
                pltpu.make_async_copy(piece, target, recv_sem.at[key]).start()

        @pl.when(jnp.logical_not(diagonal))
        def _():
            for key, piece, target in pieces():
                send(key, piece, target, dev_spot)

    def share(stream):
        for part in range(2):
            mine = rows(full_in.at[stream], token, part * half, half)
            arrived(key_of(stream, GATHER) + part, mine)
            send(key_of(stream, CROSS) + part, mine, mine, dev_cross)
        mine = rows(full_in.at[stream], token)
        send(key_of(stream, CORE), mine, mine, dev_core)

    def relay(stream):
        for part in range(2):
            theirs = rows(full_in.at[stream], token_cross, part * half, half)
            arrived(key_of(stream, CROSS) + part, theirs)
            send(key_of(stream, RELAY) + part, theirs, theirs, dev_core)

    def multiply(stream):
        arrived(key_of(stream, CORE), rows(full_in.at[stream], token_core))
        for part in range(2):
            arrived(key_of(stream, RELAY) + part, rows(full_in.at[stream], token_both, part * half, half))

        @pl.loop(0, width // tile)
        def _(step):
            at = pl.ds(pl.multiple_of(step * tile, tile), tile)
            partial[stream, :, at] = jnp.dot(
                full_in[stream], weight[:, at], preferred_element_type=F32
            ).astype(BF16)

        mine, reach, final = partial.at[stream], hop_in.at[stream], last_in.at[stream]
        send(key_of(stream, HOP_UP), rows(mine, over, 0, half), reach.at[0], dev_up)
        send(key_of(stream, HOP_DOWN), rows(mine, over, half, half), reach.at[1], dev_down)
        send(key_of(stream, LATE_UP), rows(mine, up, half, half), final.at[0, pl.ds(half, half)], dev_up)
        send(key_of(stream, LATE_DOWN), rows(mine, down, 0, half), final.at[1, pl.ds(0, half)], dev_down)

    def pass_sum(stream):
        mine, reach, final = partial.at[stream], hop_in.at[stream], last_in.at[stream]
        arrived(key_of(stream, HOP_UP), reach.at[0])
        hop_out[stream, 0] = (reach[0].astype(F32) + rows(mine, up, 0, half)[...].astype(F32)).astype(BF16)
        send(key_of(stream, SUM_UP), hop_out.at[stream, 0], final.at[0, pl.ds(0, half)], dev_up)
        arrived(key_of(stream, HOP_DOWN), reach.at[1])
        hop_out[stream, 1] = (reach[1].astype(F32) + rows(mine, down, half, half)[...].astype(F32)).astype(BF16)
        send(key_of(stream, SUM_DOWN), hop_out.at[stream, 1], final.at[1, pl.ds(half, half)], dev_down)

    def pre_activation(stream):
        final = last_in.at[stream]
        arrived(key_of(stream, LATE_UP), final.at[0, pl.ds(half, half)])
        arrived(key_of(stream, LATE_DOWN), final.at[1, pl.ds(0, half)])
        arrived(key_of(stream, SUM_UP), final.at[0, pl.ds(0, half)])
        arrived(key_of(stream, SUM_DOWN), final.at[1, pl.ds(half, half)])
        own = rows(partial.at[stream], row)[...].astype(F32)
        return own + final[0].astype(F32) + final[1].astype(F32)

    def advance(stream, own_block):
        pre = pre_activation(stream)
        return (own_block.astype(F32) + gain_ref[...] * (pre * jax.nn.sigmoid(pre))).astype(BF16)

    def scale(tick, stream, coming):
        pre = pre_activation(stream)
        sigma = jax.nn.sigmoid(pre)
        slope = sigma * (1.0 + pre * (1.0 - sigma))
        all_rows = scaled.at[tick]
        rows(all_rows, row)[...] = (coming.astype(F32) * gain_ref[...] * slope).astype(BF16)
        low, high = rows(all_rows, row, 0, half), rows(all_rows, row, half, half)
        send(back_key(tick, OWN_UP), low, low, dev_up)
        send(back_key(tick, OWN_DOWN), high, high, dev_down)
        send(back_key(tick, REST_UP), high, high, dev_up)
        send(back_key(tick, REST_DOWN), low, low, dev_down)

    def pass_scaled(tick):
        low, high = rows(scaled.at[tick], down, 0, half), rows(scaled.at[tick], up, half, half)
        arrived(back_key(tick, OWN_UP), low)
        send(back_key(tick, NEXT_UP), low, low, dev_up)
        arrived(back_key(tick, OWN_DOWN), high)
        send(back_key(tick, NEXT_DOWN), high, high, dev_down)

    def multiply_back(tick):
        all_rows = scaled.at[tick]
        arrived(back_key(tick, REST_UP), rows(all_rows, down, half, half))
        arrived(back_key(tick, REST_DOWN), rows(all_rows, up, 0, half))
        arrived(back_key(tick, NEXT_UP), rows(all_rows, over, 0, half))
        arrived(back_key(tick, NEXT_DOWN), rows(all_rows, over, half, half))

        @pl.loop(0, width // tile)
        def _(step):
            at = pl.ds(pl.multiple_of(step * tile, tile), tile)
            back_partial[tick, :, at] = lax.dot_general(
                scaled[tick], weight[at, :], (((1,), (1,)), ((), ())), preferred_element_type=F32
            ).astype(BF16)

        mine = back_partial.at[tick]
        for part in range(2):
            far = core_in.at[tick, 1, pl.ds(part * half, half)]
            send(back_key(tick, PART_FAR) + part, rows(mine, token_both, part * half, half), far, dev_core)
        send(back_key(tick, PART_NEAR), rows(mine, token_core), core_in.at[tick, 0], dev_core)

    def pair_sum(tick):
        for part in range(2):
            at = pl.ds(part * half, half)
            arrived(back_key(tick, PART_FAR) + part, core_in.at[tick, 1, at])
            own = rows(back_partial.at[tick], token_cross, part * half, half)[...].astype(F32)
            pair_out[tick, at] = (own + core_in[tick, 1, at].astype(F32)).astype(BF16)
            send(back_key(tick, PAIR) + part, pair_out.at[tick, at], pair_in.at[tick, at], dev_cross)

    def home_sum(tick):
        arrived(back_key(tick, PART_NEAR), core_in.at[tick, 0])
        for part in range(2):
            at = pl.ds(part * half, half)
            key = back_key(tick, HOME) + part
            arrived(back_key(tick, PAIR) + part, pair_in.at[tick, at])
            own = rows(back_partial.at[tick], token, part * half, half)[...].astype(F32)
            home_out[tick, at] = (own + core_in[tick, 0, at].astype(F32) + pair_in[tick, at].astype(F32)).astype(BF16)
            if tick == 0:
                send(key, home_out.at[tick, at], home_in.at[tick, at], (seg_prev, token, row))
                continue

            @pl.when(diagonal)
            def _():
                pltpu.make_async_copy(home_out.at[tick, at], home_in.at[tick, at], recv_sem.at[key]).start()

            @pl.when(jnp.logical_not(diagonal))
            def _():
                send(key, home_out.at[tick, at], home_in.at[tick, at], dev_home)

    def home_arrived(tick):
        for part in range(2):
            arrived(back_key(tick, HOME) + part, home_in.at[tick, pl.ds(part * half, half)])

    def added(coming, term):
        return (coming.astype(F32) + term.astype(F32)).astype(BF16)

    def store(at, src, dst):
        copy = pltpu.make_async_copy(src, dst, local_sem.at[at])
        copy.start()
        return copy

    def wait_loads():
        for load in loads:
            load.wait()

    stores = []

    def pass_on_output():
        result[0] = advance(FWD1, incoming[...])
        message[...] = jnp.where(seg == segments - 1, fresh[...], result[0])
        send(key_of(FWD2, GATHER), message.at[pl.ds(0, half)], rows(full_in.at[FWD2], row, 0, half), (seg_next, col, spot))
        send(key_of(FWD2, GATHER) + 1, message.at[pl.ds(half, half)], rows(full_in.at[FWD2], row, half, half), (seg_next, col, spot))
        send(SEG_OUT, message, feed, (seg_next, row, col))
        stores.append(store(5, result.at[0], both_hbm.at[0, 0]))

    def pass_on_returning():
        pl.semaphore_wait(here_sem, 2)
        send(SEG_RETURNING, returning_hbm, returning_next, (seg_prev, row, col))

    def scale_second():
        arrived(SEG_RETURNING, returning_next)
        home_arrived(0)
        following = added(returning_next[...], home_in[0])
        upstream[...] = jnp.where(seg == segments - 1, cotangent[...], following)
        scale(1, BACK2, upstream[...])
        send(SEG_TERM, home_in.at[0], term, (seg_next, row, col))

    def finish_first():
        arrived(SEG_TERM, term)
        grad[0] = added(returning[...], term[...])
        stores.append(store(6, grad.at[0], both_hbm.at[1, 0]))

    def finish_output():
        arrived(SEG_OUT, feed)
        result[1] = advance(FWD2, feed[...])
        stores.append(store(7, result.at[1], both_hbm.at[0, 1]))

    def finish_gradient():
        home_arrived(1)
        grad[1] = added(upstream[...], home_in[1])
        stores.append(store(8, grad.at[1], both_hbm.at[1, 1]))

    gather(BACK1, stash_hbm.at[0])
    gather(FWD1, incoming_hbm)
    share(BACK1)
    gather(BACK2, stash_hbm.at[1])
    share(FWD1)
    relay(BACK1)
    wait_loads()
    multiply(BACK1)
    relay(FWD1)
    share(BACK2)
    multiply(FWD1)
    pass_sum(BACK1)
    relay(BACK2)
    pass_sum(FWD1)
    scale(0, BACK1, returning[...])
    multiply(BACK2)
    pass_on_returning()
    pass_scaled(0)
    pass_on_output()
    multiply_back(0)
    pair_sum(0)
    pass_sum(BACK2)
    home_sum(0)
    share(FWD2)
    scale_second()
    relay(FWD2)
    pass_scaled(1)
    multiply(FWD2)
    multiply_back(1)
    pass_sum(FWD2)
    pair_sum(1)
    finish_first()
    home_sum(1)
    finish_output()
    finish_gradient()

    around = [key_of(stream, GATHER) + part for stream in (BACK1, FWD1, BACK2) for part in range(2)]
    around += [back_key(1, HOME) + part for part in range(2)]
    for key, is_half in sent.items():
        if key not in around:
            left(key, hop_in.at[0, 0] if is_half else home_in.at[0])

    @pl.when(jnp.logical_not(diagonal))
    def _():
        for key in around:
            left(key, hop_in.at[0, 0])

    for copy in stores:
        copy.wait()


def relay_call(segments, weights, gains, incoming, fresh, returning, cotangent, stashed):
    block, width = incoming.shape
    half, tokens = block // 2, 4 * block
    piece = (block, width)
    hbm = pl.BlockSpec(memory_space=pl.ANY)
    vmem = lambda *shape: pltpu.VMEM(shape, BF16)
    return pl.pallas_call(
        functools.partial(kernel, segments),
        out_shape=jax.ShapeDtypeStruct((2, 2) + piece, BF16),
        in_specs=[pl.BlockSpec(memory_space=pltpu.VMEM)] + [hbm] * 6,
        out_specs=hbm,
        scratch_shapes=[
            vmem(width, width),
            vmem(*piece),
            vmem(*piece),
            vmem(*piece),
            vmem(*piece),
            vmem(4, tokens, width),
            vmem(4, tokens, width),
            vmem(4, 2, half, width),
            vmem(4, 2, half, width),
            vmem(4, 2, block, width),
            vmem(2, tokens, width),
            vmem(2, tokens, width),
            vmem(2, 2, block, width),
            vmem(2, block, width),
            vmem(2, block, width),
            vmem(2, block, width),
            vmem(2, block, width),
            vmem(2, block, width),
            vmem(*piece),
            vmem(*piece),
            vmem(*piece),
            vmem(2, block, width),
            vmem(*piece),
            vmem(*piece),
            pltpu.SemaphoreType.DMA((COPIES,)),
            pltpu.SemaphoreType.DMA((COPIES,)),
            pltpu.SemaphoreType.DMA((9,)),
            pltpu.SemaphoreType.REGULAR,
        ],
        compiler_params=pltpu.CompilerParams(collective_id=0, has_side_effects=True),
    )(gains, weights, incoming, fresh, returning, cotangent, stashed)


def solution(mesh):
    segments = mesh.shape["segment"]

    def shards(weights, layer_gains, incoming, fresh_batch, returning, fresh_cotangent, stashed_inputs):
        both = relay_call(
            segments,
            weights[0],
            layer_gains,
            incoming[0],
            fresh_batch,
            returning[0],
            fresh_cotangent,
            stashed_inputs[0],
        )
        return both[0][None], both[1][None]

    in_specs = (
        P("segment", "row", "col"),
        P("segment", "col"),
        P("segment", "row", "col"),
        P("row", "col"),
        P("segment", "row", "col"),
        P("row", "col"),
        P("segment", None, "row", "col"),
    )
    out_specs = (P("segment", None, "row", "col"), P("segment", None, "row", "col"))
    return jax.shard_map(shards, mesh=mesh, in_specs=in_specs, out_specs=out_specs, check_vma=False)
```

```python
import functools

import jax
import jax.numpy as jnp
from jax import lax
from jax.experimental import pallas as pl
from jax.experimental.pallas import tpu as pltpu
from jax.sharding import PartitionSpec as P

MESH = pl.DeviceIdType.MESH
BF16 = jnp.bfloat16
F32 = jnp.float32

BACK1, FWD1, BACK2, FWD2 = range(4)
GATHER, CROSS, RELAY, CORE, HOP_UP, HOP_DOWN, LATE_UP, LATE_DOWN, SUM_UP, SUM_DOWN = 0, 2, 4, 6, 7, 8, 9, 10, 11, 12
STREAM_COPIES = 13
OWN_UP, OWN_DOWN, REST_UP, REST_DOWN, NEXT_UP, NEXT_DOWN, PART_NEAR, PART_FAR, PAIR, HOME = 0, 1, 2, 3, 4, 5, 6, 7, 9, 11
BACK_COPIES = 13
BACK_START = 4 * STREAM_COPIES
SEG_OUT = BACK_START + 2 * BACK_COPIES
SEG_RETURNING, SEG_TERM = SEG_OUT + 1, SEG_OUT + 2
COPIES = SEG_OUT + 3


def token_of(row, col):
    first = jnp.where(col == 0, 0, jnp.where(col == 1, 3, col - 1))
    last = jnp.where(col == 2, 0, jnp.where(col == 3, 3, col + 1))
    return jnp.where(row == 0, first, jnp.where(row == 3, last, col))


def collector_of(row, token):
    first = jnp.where(token == 0, 0, jnp.where(token == 3, 1, token + 1))
    last = jnp.where(token == 0, 2, jnp.where(token == 3, 3, token - 1))
    return jnp.where(row == 0, first, jnp.where(row == 3, last, token))


def kernel(
    segments,
    gain_ref,
    weight_hbm,
    incoming_hbm,
    fresh_hbm,
    returning_hbm,
    cotangent_hbm,
    stash_hbm,
    both_hbm,
    weight,
    incoming,
    fresh,
    returning,
    cotangent,
    full_in,
    partial,
    hop_in,
    hop_out,
    last_in,
    scaled,
    back_partial,
    core_in,
    pair_out,
    pair_in,
    home_out,
    home_in,
    result,
    message,
    feed,
    upstream,
    grad,
    returning_next,
    term,
    send_sem,
    recv_sem,
    local_sem,
    here_sem,
):
    seg = lax.axis_index("segment")
    row = lax.axis_index("row")
    col = lax.axis_index("col")
    block = incoming.shape[0]
    half = block // 2
    width = incoming.shape[1]
    tile = min(256, width)

    up, down, over = (row + 1) % 4, (row + 3) % 4, (row + 2) % 4
    core = col + 1 - 2 * (col % 2)
    cross = (col + 2) % 4
    both = (core + 2) % 4
    token, token_core, token_cross, token_both = [token_of(row, c) for c in (col, core, cross, both)]
    spot = collector_of(col, row)
    seg_next = (seg + 1) % segments
    seg_prev = (seg + segments - 1) % segments
    diagonal = row == col

    dev_core, dev_cross = (seg, row, core), (seg, row, cross)
    dev_up, dev_down = (seg, up, col), (seg, down, col)
    dev_spot, dev_home = (seg, col, spot), (seg, token, row)

    def rows(ref, index, start=0, size=None):
        size = block if size is None else size
        return ref.at[pl.ds(pl.multiple_of(index * block + start, half), size)]

    sent = {}

    def send(key, src, dst, device):
        sent[key] = dst.shape[0] == half
        copy = pltpu.make_async_remote_copy(
            src_ref=src,
            dst_ref=dst,
            send_sem=send_sem.at[key],
            recv_sem=recv_sem.at[key],
            device_id=device,
            device_id_type=MESH,
        )
        copy.start()

    def arrived(key, ref):
        pltpu.make_async_remote_copy(
            src_ref=ref,
            dst_ref=ref,
            send_sem=send_sem.at[key],
            recv_sem=recv_sem.at[key],
            device_id=dev_core,
            device_id_type=MESH,
        ).wait_recv()

    def left(key, ref):
        pltpu.make_async_remote_copy(
            src_ref=ref,
            dst_ref=ref,
            send_sem=send_sem.at[key],
            recv_sem=recv_sem.at[key],
            device_id=dev_core,
            device_id_type=MESH,
        ).wait_send()

    loads = [
        pltpu.make_async_copy(src, dst, local_sem.at[at])
        for at, (src, dst) in enumerate(
            [
                (weight_hbm, weight),
                (incoming_hbm, incoming),
                (returning_hbm, returning),
                (fresh_hbm, fresh),
                (cotangent_hbm, cotangent),
            ]
        )
    ]
    for load in loads:
        load.start()

    barrier = pltpu.get_barrier_semaphore()
    others = [dev_core, dev_cross, dev_up, dev_down, (seg_prev, row, col), (seg_prev, token, row)]
    for device in others:
        pl.semaphore_signal(barrier, inc=1, device_id=device, device_id_type=MESH)

    @pl.when(diagonal)
    def _():
        pl.semaphore_wait(barrier, len(others))

    @pl.when(jnp.logical_not(diagonal))
    def _():
        for device in (dev_spot, dev_home):
            pl.semaphore_signal(barrier, inc=1, device_id=device, device_id_type=MESH)
        pl.semaphore_wait(barrier, len(others) + 2)

    for device in ((seg_next, row, col), (seg_next, col, spot)):
        pl.semaphore_signal(here_sem, inc=1, device_id=device, device_id_type=MESH)

    def key_of(stream, step):
        return stream * STREAM_COPIES + step

    def back_key(tick, step):
        return BACK_START + tick * BACK_COPIES + step

    def gather(stream, source):
        def pieces():
            for part in range(2):
                piece = source.at[pl.ds(part * half, half)]
                yield key_of(stream, GATHER) + part, piece, rows(full_in.at[stream], row, part * half, half)

        @pl.when(diagonal)
        def _():
            for key, piece, target in pieces():
                pltpu.make_async_copy(piece, target, recv_sem.at[key]).start()

        @pl.when(jnp.logical_not(diagonal))
        def _():
            for key, piece, target in pieces():
                send(key, piece, target, dev_spot)

    def share(stream):
        for part in range(2):
            mine = rows(full_in.at[stream], token, part * half, half)
            arrived(key_of(stream, GATHER) + part, mine)
            send(key_of(stream, CROSS) + part, mine, mine, dev_cross)
        mine = rows(full_in.at[stream], token)
        send(key_of(stream, CORE), mine, mine, dev_core)

    def relay(stream):
        for part in range(2):
            theirs = rows(full_in.at[stream], token_cross, part * half, half)
            arrived(key_of(stream, CROSS) + part, theirs)
            send(key_of(stream, RELAY) + part, theirs, theirs, dev_core)

    def multiply(stream):
        arrived(key_of(stream, CORE), rows(full_in.at[stream], token_core))
        for part in range(2):
            arrived(key_of(stream, RELAY) + part, rows(full_in.at[stream], token_both, part * half, half))

        @pl.loop(0, width // tile)
        def _(step):
            at = pl.ds(pl.multiple_of(step * tile, tile), tile)
            partial[stream, :, at] = jnp.dot(
                full_in[stream], weight[:, at], preferred_element_type=F32
            ).astype(BF16)

        mine, reach, final = partial.at[stream], hop_in.at[stream], last_in.at[stream]
        send(key_of(stream, HOP_UP), rows(mine, over, 0, half), reach.at[0], dev_up)
        send(key_of(stream, HOP_DOWN), rows(mine, over, half, half), reach.at[1], dev_down)
        send(key_of(stream, LATE_UP), rows(mine, up, half, half), final.at[0, pl.ds(half, half)], dev_up)
        send(key_of(stream, LATE_DOWN), rows(mine, down, 0, half), final.at[1, pl.ds(0, half)], dev_down)

    def pass_sum(stream):
        mine, reach, final = partial.at[stream], hop_in.at[stream], last_in.at[stream]
        arrived(key_of(stream, HOP_UP), reach.at[0])
        hop_out[stream, 0] = (reach[0].astype(F32) + rows(mine, up, 0, half)[...].astype(F32)).astype(BF16)
        send(key_of(stream, SUM_UP), hop_out.at[stream, 0], final.at[0, pl.ds(0, half)], dev_up)
        arrived(key_of(stream, HOP_DOWN), reach.at[1])
        hop_out[stream, 1] = (reach[1].astype(F32) + rows(mine, down, half, half)[...].astype(F32)).astype(BF16)
        send(key_of(stream, SUM_DOWN), hop_out.at[stream, 1], final.at[1, pl.ds(half, half)], dev_down)

    def pre_activation(stream):
        final = last_in.at[stream]
        arrived(key_of(stream, LATE_UP), final.at[0, pl.ds(half, half)])
        arrived(key_of(stream, LATE_DOWN), final.at[1, pl.ds(0, half)])
        arrived(key_of(stream, SUM_UP), final.at[0, pl.ds(0, half)])
        arrived(key_of(stream, SUM_DOWN), final.at[1, pl.ds(half, half)])
        own = rows(partial.at[stream], row)[...].astype(F32)
        return own + final[0].astype(F32) + final[1].astype(F32)

    def advance(stream, own_block):
        pre = pre_activation(stream)
        return (own_block.astype(F32) + gain_ref[...] * (pre * jax.nn.sigmoid(pre))).astype(BF16)

    def scale(tick, stream, coming):
        final, all_rows = last_in.at[stream], scaled.at[tick]
        for part, keys in enumerate(((SUM_UP, LATE_DOWN), (LATE_UP, SUM_DOWN))):
            at = pl.ds(part * half, half)
            for side, key in enumerate(keys):
                arrived(key_of(stream, key), final.at[side, at])
            own = rows(partial.at[stream], row, part * half, half)[...].astype(F32)
            pre = own + final[0, at].astype(F32) + final[1, at].astype(F32)
            sigma = jax.nn.sigmoid(pre)
            slope = sigma * (1.0 + pre * (1.0 - sigma))
            came = coming[part * half : (part + 1) * half].astype(F32)
            piece = rows(all_rows, row, part * half, half)
            piece[...] = (came * gain_ref[...] * slope).astype(BF16)
            send(back_key(tick, (OWN_UP, OWN_DOWN)[part]), piece, piece, (dev_up, dev_down)[part])
        low, high = rows(all_rows, row, 0, half), rows(all_rows, row, half, half)
        send(back_key(tick, REST_UP), high, high, dev_up)
        send(back_key(tick, REST_DOWN), low, low, dev_down)

    def pass_scaled(tick):
        low, high = rows(scaled.at[tick], down, 0, half), rows(scaled.at[tick], up, half, half)
        arrived(back_key(tick, OWN_UP), low)
        send(back_key(tick, NEXT_UP), low, low, dev_up)
        arrived(back_key(tick, OWN_DOWN), high)
        send(back_key(tick, NEXT_DOWN), high, high, dev_down)

    def multiply_back(tick):
        all_rows = scaled.at[tick]
        arrived(back_key(tick, REST_UP), rows(all_rows, down, half, half))
        arrived(back_key(tick, REST_DOWN), rows(all_rows, up, 0, half))
        arrived(back_key(tick, NEXT_UP), rows(all_rows, over, 0, half))
        arrived(back_key(tick, NEXT_DOWN), rows(all_rows, over, half, half))

        @pl.loop(0, width // tile)
        def _(step):
            at = pl.ds(pl.multiple_of(step * tile, tile), tile)
            back_partial[tick, :, at] = lax.dot_general(
                scaled[tick], weight[at, :], (((1,), (1,)), ((), ())), preferred_element_type=F32
            ).astype(BF16)

        mine = back_partial.at[tick]
        for part in range(2):
            far = core_in.at[tick, 1, pl.ds(part * half, half)]
            send(back_key(tick, PART_FAR) + part, rows(mine, token_both, part * half, half), far, dev_core)
        send(back_key(tick, PART_NEAR), rows(mine, token_core), core_in.at[tick, 0], dev_core)

    def pair_sum(tick):
        for part in range(2):
            at = pl.ds(part * half, half)
            arrived(back_key(tick, PART_FAR) + part, core_in.at[tick, 1, at])
            own = rows(back_partial.at[tick], token_cross, part * half, half)[...].astype(F32)
            pair_out[tick, at] = (own + core_in[tick, 1, at].astype(F32)).astype(BF16)
            send(back_key(tick, PAIR) + part, pair_out.at[tick, at], pair_in.at[tick, at], dev_cross)

    def home_sum(tick):
        arrived(back_key(tick, PART_NEAR), core_in.at[tick, 0])
        for part in range(2):
            at = pl.ds(part * half, half)
            key = back_key(tick, HOME) + part
            arrived(back_key(tick, PAIR) + part, pair_in.at[tick, at])
            own = rows(back_partial.at[tick], token, part * half, half)[...].astype(F32)
            home_out[tick, at] = (own + core_in[tick, 0, at].astype(F32) + pair_in[tick, at].astype(F32)).astype(BF16)
            if tick == 0:
                send(key, home_out.at[tick, at], home_in.at[tick, at], (seg_prev, token, row))
                continue

            @pl.when(diagonal)
            def _():
                pltpu.make_async_copy(home_out.at[tick, at], home_in.at[tick, at], recv_sem.at[key]).start()

            @pl.when(jnp.logical_not(diagonal))
            def _():
                send(key, home_out.at[tick, at], home_in.at[tick, at], dev_home)

    def home_arrived(tick):
        for part in range(2):
            arrived(back_key(tick, HOME) + part, home_in.at[tick, pl.ds(part * half, half)])

    def added(coming, term):
        return (coming.astype(F32) + term.astype(F32)).astype(BF16)

    def store(at, src, dst):
        copy = pltpu.make_async_copy(src, dst, local_sem.at[at])
        copy.start()
        return copy

    def wait_loads():
        for load in loads:
            load.wait()

    stores = []

    def pass_on_output():
        result[0] = advance(FWD1, incoming[...])
        message[...] = jnp.where(seg == segments - 1, fresh[...], result[0])
        send(key_of(FWD2, GATHER), message.at[pl.ds(0, half)], rows(full_in.at[FWD2], row, 0, half), (seg_next, col, spot))
        send(key_of(FWD2, GATHER) + 1, message.at[pl.ds(half, half)], rows(full_in.at[FWD2], row, half, half), (seg_next, col, spot))
        send(SEG_OUT, message, feed, (seg_next, row, col))
        stores.append(store(5, result.at[0], both_hbm.at[0, 0]))

    def pass_on_returning():
        pl.semaphore_wait(here_sem, 2)
        send(SEG_RETURNING, returning_hbm, returning_next, (seg_prev, row, col))

    def scale_second():
        arrived(SEG_RETURNING, returning_next)
        home_arrived(0)
        following = added(returning_next[...], home_in[0])
        upstream[...] = jnp.where(seg == segments - 1, cotangent[...], following)
        scale(1, BACK2, upstream[...])
        send(SEG_TERM, home_in.at[0], term, (seg_next, row, col))

    def finish_first():
        arrived(SEG_TERM, term)
        grad[0] = added(returning[...], term[...])
        stores.append(store(6, grad.at[0], both_hbm.at[1, 0]))

    def finish_output():
        arrived(SEG_OUT, feed)
        result[1] = advance(FWD2, feed[...])
        stores.append(store(7, result.at[1], both_hbm.at[0, 1]))

    def finish_gradient():
        home_arrived(1)
        grad[1] = added(upstream[...], home_in[1])
        stores.append(store(8, grad.at[1], both_hbm.at[1, 1]))

    gather(BACK1, stash_hbm.at[0])
    gather(FWD1, incoming_hbm)
    share(BACK1)
    gather(BACK2, stash_hbm.at[1])
    share(FWD1)
    relay(BACK1)
    wait_loads()
    multiply(BACK1)
    relay(FWD1)
    share(BACK2)
    pass_sum(BACK1)
    multiply(FWD1)
    relay(BACK2)
    pass_sum(FWD1)
    scale(0, BACK1, returning[...])
    multiply(BACK2)
    pass_on_returning()
    pass_scaled(0)
    pass_on_output()
    multiply_back(0)
    pair_sum(0)
    pass_sum(BACK2)
    home_sum(0)
    share(FWD2)
    scale_second()
    relay(FWD2)
    pass_scaled(1)
    multiply(FWD2)
    multiply_back(1)
    pair_sum(1)
    pass_sum(FWD2)
    home_sum(1)
    finish_first()
    finish_output()
    finish_gradient()

    around = [key_of(stream, GATHER) + part for stream in (BACK1, FWD1, BACK2) for part in range(2)]
    around += [back_key(1, HOME) + part for part in range(2)]
    for key, is_half in sent.items():
        if key not in around:
            left(key, hop_in.at[0, 0] if is_half else home_in.at[0])

    @pl.when(jnp.logical_not(diagonal))
    def _():
        for key in around:
            left(key, hop_in.at[0, 0])

    for copy in stores:
        copy.wait()


def relay_call(segments, weights, gains, incoming, fresh, returning, cotangent, stashed):
    block, width = incoming.shape
    half, tokens = block // 2, 4 * block
    piece = (block, width)
    hbm = pl.BlockSpec(memory_space=pl.ANY)
    vmem = lambda *shape: pltpu.VMEM(shape, BF16)
    return pl.pallas_call(
        functools.partial(kernel, segments),
        out_shape=jax.ShapeDtypeStruct((2, 2) + piece, BF16),
        in_specs=[pl.BlockSpec(memory_space=pltpu.VMEM)] + [hbm] * 6,
        out_specs=hbm,
        scratch_shapes=[
            vmem(width, width),
            vmem(*piece),
            vmem(*piece),
            vmem(*piece),
            vmem(*piece),
            vmem(4, tokens, width),
            vmem(4, tokens, width),
            vmem(4, 2, half, width),
            vmem(4, 2, half, width),
            vmem(4, 2, block, width),
            vmem(2, tokens, width),
            vmem(2, tokens, width),
            vmem(2, 2, block, width),
            vmem(2, block, width),
            vmem(2, block, width),
            vmem(2, block, width),
            vmem(2, block, width),
            vmem(2, block, width),
            vmem(*piece),
            vmem(*piece),
            vmem(*piece),
            vmem(2, block, width),
            vmem(*piece),
            vmem(*piece),
            pltpu.SemaphoreType.DMA((COPIES,)),
            pltpu.SemaphoreType.DMA((COPIES,)),
            pltpu.SemaphoreType.DMA((9,)),
            pltpu.SemaphoreType.REGULAR,
        ],
        compiler_params=pltpu.CompilerParams(collective_id=0, has_side_effects=True),
    )(gains, weights, incoming, fresh, returning, cotangent, stashed)


def solution(mesh):
    segments = mesh.shape["segment"]

    def shards(weights, layer_gains, incoming, fresh_batch, returning, fresh_cotangent, stashed_inputs):
        both = relay_call(
            segments,
            weights[0],
            layer_gains,
            incoming[0],
            fresh_batch,
            returning[0],
            fresh_cotangent,
            stashed_inputs[0],
        )
        return both[0][None], both[1][None]

    in_specs = (
        P("segment", "row", "col"),
        P("segment", "col"),
        P("segment", "row", "col"),
        P("row", "col"),
        P("segment", "row", "col"),
        P("row", "col"),
        P("segment", None, "row", "col"),
    )
    out_specs = (P("segment", None, "row", "col"), P("segment", None, "row", "col"))
    return jax.shard_map(shards, mesh=mesh, in_specs=in_specs, out_specs=out_specs, check_vma=False)
```
